256 devices in a mesh: dp: 8 (over y, x_lo), tensor: 32 (over x_hi, z, core).
Axes of the slice: x: 4 (x_hi: 2, x_lo: 2; x = x_hi * 2 + x_lo), y: 4, z: 8, core: 2. Of those that a mesh axis runs over, the one named last changes fastest.
Arguments:
- hidden: bfloat16 [6144, 20480], P('dp', 'tensor'), may hold values from -6 to 6
- out_grad: bfloat16 [6144, 8192], P('dp', 'tensor'), may hold values from -6 to 6
- w_down: bfloat16 [20480, 8192], P('tensor'), may hold values from -0.0625 to 0.0625
- proj_in: bfloat16 [64, 20480], P(None, 'tensor'), may hold values from -0.0390625 to 0.0390625
- proj_out: bfloat16 [64, 8192], P(None, 'tensor'), may hold values from -0.0625 to 0.0625
- queries: bfloat16 [1024, 4096], P('tensor'), may hold values from -0.005859375 to 0.005859375
- assignment: int32 [24], replicated, may hold values from 0 to 15
Outputs:
- input_grad: bfloat16 [6144, 20480], P('dp', 'tensor')
- scores: float32 [16, 1024], P('dp', 'tensor')
The draws below stay inside these ranges and needn't reach their ends.
All inputs are finite; a program needn't handle non-finite values.
Results may differ from the reference program's by a relative error of at most 0.001.
Values may be sent and summed in bfloat16 or wider, within the bound.
No kernel may reach another device: no remote copies, remote signals or barrier semaphores. Data moves between devices by JAX's collectives and lax.ppermute only.
A program may use at most 128 MiB of HBM per device.

```python
import jax
import jax.numpy as jnp
from jax import lax

D = 8192
FF = 20480
K = 64
LEN = 256
Q = 1024
SEQS = 24
TOKENS = 6144
EXAMPLES = 16


def with_ends(array, key, low, high):
    extent = array.shape
    place = [jax.random.randint(jax.random.fold_in(key, axis), (), 0, extent[axis]) for axis in range(len(extent))]
    array = array.at[tuple(place)].set(low)
    longest = extent.index(max(extent))
    place[longest] = (place[longest] + 1) % extent[longest]
    return array.at[tuple(place)].set(high)


def steps_of(own_key, dims, shards, least, high):
    gain = 1.0
    for position, blocks in shards:
        heights = jax.random.uniform(jax.random.fold_in(jax.random.fold_in(own_key, 6), position), (blocks,), jnp.float32, least / len(shards), high / len(shards))
        gain = gain * jnp.repeat(jnp.exp(heights), dims[position] // blocks).reshape((-1,) + (1,) * (len(dims) - 1 - position))
    return gain


def gaussian(stream_key, shape, spread, most, shards=(), kind=jnp.bfloat16):
    drawn = jax.random.normal(stream_key, shape, jnp.float32) * spread
    if len(shards) > 0:
        drawn = steps_of(stream_key, shape, shards, -0.22, 0.18) * drawn
    return jnp.clip(drawn, min=-most, max=most).astype(kind)


def setup_inputs(seed: int = 0) -> dict:
    keys = jax.random.split(jax.random.key(seed), 8)
    return {
        "hidden": gaussian(keys[0], (TOKENS, FF), 1.0, 6.0, ((0, 8), (1, 32))),
        "out_grad": gaussian(keys[1], (TOKENS, D), 1.0, 6.0, ((0, 8), (1, 32))),
        "w_down": gaussian(keys[2], (FF, D), D ** -0.5, 0.0625, ((0, 32),)),
        "proj_in": gaussian(keys[3], (K, FF), FF ** -0.5, 0.0390625, ((1, 32),)),
        "proj_out": gaussian(keys[4], (K, D), D ** -0.5, 0.0625, ((1, 32),)),
        "queries": gaussian(keys[5], (Q, K * K), (K * K * LEN) ** -0.5, 0.005859375, ((0, 32),)),
        "assignment": with_ends(jax.random.randint(keys[6], (SEQS,), 0, EXAMPLES), jax.random.fold_in(keys[6], 1), 0, EXAMPLES - 1).astype(jnp.int32),
    }


def reference(hidden, out_grad, w_down, proj_in, proj_out, queries, assignment):
    input_grad = jnp.dot(out_grad, w_down.T, preferred_element_type=jnp.float32).astype(jnp.bfloat16)
    act_low = jnp.dot(hidden, proj_in.T, preferred_element_type=jnp.float32)
    grad_low = jnp.dot(out_grad, proj_out.T, preferred_element_type=jnp.float32)
    act_seq = act_low.reshape(SEQS, LEN, K)
    grad_seq = grad_low.reshape(SEQS, LEN, K)
    seq_grads = jnp.einsum("slk,slm->skm", act_seq, grad_seq, precision=lax.Precision.HIGHEST).reshape(SEQS, K * K)
    one_hot = (assignment[:, None] == jnp.arange(EXAMPLES, dtype=jnp.int32)[None, :]).astype(jnp.float32)
    example_grads = jnp.dot(one_hot.T, seq_grads, precision=lax.Precision.HIGHEST)
    scores = jnp.dot(example_grads, queries.astype(jnp.float32).T, precision=lax.Precision.HIGHEST)
    return input_grad, scores
```

```python
import jax
import jax.numpy as jnp
from jax import lax
from jax.sharding import PartitionSpec as P

LEN = 256
EX_DEV = 2
DP = 8
TENSOR = 32
ZN = 8


def place(xh, z, c):
    return xh * 16 + (z % ZN) * 2 + c


def pairs(move):
    out = []
    for xh in range(2):
        for z in range(ZN):
            for c in range(2):
                out.append((place(xh, z, c), place(*move(xh, z, c))))
    return out


CORE = pairs(lambda xh, z, c: (xh, z, 1 - c))
ACROSS = pairs(lambda xh, z, c: (1 - xh, z, c))
ALONG = pairs(lambda xh, z, c: (xh, z + 1 - 2 * c, c))
Z_GROUPS = [[place(xh, z, c) for z in range(ZN)] for xh in range(2) for c in range(2)]


def move(value, perm):
    return lax.ppermute(value, "tensor", perm)


def mul(rows, weights):
    return lax.dot_general(rows, weights, (((1,), (1,)), ((), ())), preferred_element_type=jnp.float32)


def on_device(hidden, out_grad, w_down, proj_in, proj_out, queries, assignment):
    rank = lax.axis_index("tensor")
    core = rank & 1
    z = (rank >> 1) & (ZN - 1)
    xh = rank >> 4
    toward = 1 - 2 * core
    width = out_grad.shape[1]

    def weights(column, depth):
        chip = column * ZN + ((depth + 2 * ZN) & (ZN - 1))
        return lax.dynamic_slice(w_down, (0, chip * 2 * width), (w_down.shape[0], 2 * width))

    def both(own, other):
        return jnp.where(core == 0, jnp.concatenate([own, other], 1), jnp.concatenate([other, own], 1))

    own_col = both(out_grad, move(out_grad, CORE))
    crossed = move(out_grad, ACROSS)
    other_col = both(crossed, move(crossed, CORE))

    act_part = mul(hidden, proj_in)
    grad_part = mul(out_grad, proj_out)
    low = jnp.concatenate([act_part, grad_part], 1)
    seq_count = low.shape[0] // LEN
    wide = low.shape[1]
    low = low.reshape(seq_count, LEN, wide)

    def halve(value, bit, perm):
        half = value.shape[1] // 2
        keep = lax.dynamic_slice_in_dim(value, bit * half, half, 1)
        give = lax.dynamic_slice_in_dim(value, (1 - bit) * half, half, 1)
        return keep + move(give, perm)

    low = halve(low, core, CORE)
    low = halve(low, xh, ACROSS)
    share = low.shape[1] // ZN
    low = low.reshape(seq_count, ZN, share, wide).transpose(1, 0, 2, 3)
    low = lax.all_to_all(low, "tensor", 0, 0, axis_index_groups=Z_GROUPS, tiled=True)
    low = jnp.sum(low, 0)
    low = jnp.broadcast_to(low[None], (ZN,) + low.shape)
    low = lax.all_to_all(low, "tensor", 0, 0, axis_index_groups=Z_GROUPS, tiled=True)
    low = low.transpose(1, 0, 2, 3).reshape(seq_count, ZN * share, wide)
    half = wide // 2
    seq_grads = jnp.einsum(
        "slk,slm->skm", low[:, :, :half], low[:, :, half:], precision=lax.Precision.HIGHEST
    ).reshape(seq_count, half * half)
    first_seq = lax.axis_index("dp") * seq_count
    mine = lax.dynamic_slice_in_dim(assignment, first_seq, seq_count, 0)
    ids = jnp.arange(DP * EX_DEV, dtype=jnp.int32)
    one_hot = (ids[:, None] == mine[None, :]).astype(jnp.float32)
    sent = jnp.sum(one_hot[:, :, None] * seq_grads[None], 1)
    sent = sent.reshape(DP, EX_DEV, half * half)
    got = lax.all_to_all(sent, "dp", 0, 0, tiled=True)
    example_grads = jnp.sum(got, 0)
    example_grads = example_grads + move(example_grads, ACROSS)
    example_grads = example_grads + move(example_grads, CORE)
    scores = jnp.dot(example_grads, queries.astype(jnp.float32).T, precision=lax.Precision.HIGHEST)

    total = mul(own_col, weights(xh, z)) + mul(other_col, weights(1 - xh, z))
    for step in range(1, 4):
        own_col = move(own_col, ALONG)
        other_col = move(other_col, ALONG)
        own_swap = move(own_col, CORE)
        other_swap = move(other_col, CORE)
        total = total + mul(own_col, weights(xh, z - step * toward))
        total = total + mul(other_col, weights(1 - xh, z - step * toward))
        total = total + mul(own_swap, weights(xh, z + step * toward))
        total = total + mul(other_swap, weights(1 - xh, z + step * toward))
    own_half = move(lax.dynamic_slice_in_dim(own_col, core * width, width, 1), ALONG)
    other_half = move(lax.dynamic_slice_in_dim(other_col, core * width, width, 1), ALONG)
    own_col = both(own_half, move(own_half, CORE))
    other_col = both(other_half, move(other_half, CORE))
    total = total + mul(own_col, weights(xh, z + 4))
    total = total + mul(other_col, weights(1 - xh, z + 4))
    return (total.astype(jnp.bfloat16), scores)


def solution(mesh):
    placed = (
        P("dp", "tensor"),
        P("dp", "tensor"),
        P("tensor", None),
        P(None, "tensor"),
        P(None, "tensor"),
        P("tensor", None),
        P(),
    )
    return jax.shard_map(
        on_device,
        mesh=mesh,
        in_specs=placed,
        out_specs=(P("dp", "tensor"), P("dp", "tensor")),
        check_vma=False,
    )
```

```python
import jax
import jax.numpy as jnp
from jax import lax
from jax.experimental import pallas as pl
from jax.experimental.pallas import tpu as pltpu
from jax.sharding import PartitionSpec as P

LEN = 256
EX_DEV = 2
DP = 8
TENSOR = 32
ZN = 8


def place(xh, z, c):
    return xh * 16 + (z % ZN) * 2 + c


def pairs(move):
    out = []
    for xh in range(2):
        for z in range(ZN):
            for c in range(2):
                out.append((place(xh, z, c), place(*move(xh, z, c))))
    return out


CORE = pairs(lambda xh, z, c: (xh, z, 1 - c))
ACROSS = pairs(lambda xh, z, c: (1 - xh, z, c))
ALONG = pairs(lambda xh, z, c: (xh, z + 1 - 2 * c, c))
Z_GROUPS = [[place(xh, z, c) for z in range(ZN)] for xh in range(2) for c in range(2)]


def move(value, perm):
    return lax.ppermute(value, "tensor", perm)


def mul(rows, weights):
    return lax.dot_general(rows, weights, (((1,), (1,)), ((), ())), preferred_element_type=jnp.float32)


def chunk_matmul(total, pieces, blocks, w_down, out_type):
    count = len(pieces)
    rows = pieces[0].shape[0]
    widths = [piece.shape[1] for piece in pieces]
    width = max(widths)
    unit = min(widths + [width // 2])
    outs = w_down.shape[0]
    tile = rows // 2
    started = total is not None

    def kernel(blocks_ref, *refs):
        piece_refs = refs[:count]
        w_ref = refs[count]
        total_ref = refs[count + 1] if started else None
        out_ref, x_buf, w_buf, sum_buf, old_buf, x_sem, w_sem, old_sem = refs[count + 1 + started:]
        x_copies = []
        w_copies = []
        for n in range(count):
            wide = widths[n]
            start = pl.multiple_of(blocks_ref[n] * unit, unit)
            x_copies.append(pltpu.make_async_copy(piece_refs[n], x_buf.at[n, :, pl.ds(0, wide)], x_sem.at[n]))
            w_copies.append(
                pltpu.make_async_copy(w_ref.at[:, pl.ds(start, wide)], w_buf.at[n, :, pl.ds(0, wide)], w_sem.at[n])
            )
        old_copy = pltpu.make_async_copy(total_ref, old_buf, old_sem) if started else None
        merge = min(1, count - 1)
        for n in range(count):
            w_copies[n].start()
            x_copies[n].start()
            if n == merge and started:
                old_copy.start()
        for n in range(count):
            x_copies[n].wait()
            w_copies[n].wait()
            last = n + 1 == count
            with_old = started and n == merge
            if with_old:
                old_copy.wait()

            def step(i, carry, n=n, last=last, with_old=with_old):
                at = pl.ds(pl.multiple_of(i * tile, tile), tile)
                part = mul(x_buf[n, at, pl.ds(0, widths[n])], w_buf[n, :, pl.ds(0, widths[n])])
                if n > 0:
                    part = part + sum_buf[at, :]
                if with_old:
                    part = part + old_buf[at, :]
                if last:
                    out_ref[at, :] = part.astype(out_type)
                else:
                    sum_buf[at, :] = part
                return carry

            lax.fori_loop(0, rows // tile, step, 0)

    anywhere = pl.BlockSpec(memory_space=pl.ANY)
    old = [total] if started else []
    return pl.pallas_call(
        kernel,
        out_shape=jax.ShapeDtypeStruct((rows, outs), out_type),
        in_specs=[pl.BlockSpec(memory_space=pltpu.SMEM)] + [anywhere] * (count + 1 + len(old)),
        out_specs=pl.BlockSpec(memory_space=pltpu.VMEM),
        scratch_shapes=[
            pltpu.VMEM((count, rows, width), jnp.bfloat16),
            pltpu.VMEM((count, outs, width), jnp.bfloat16),
            pltpu.VMEM((rows, outs), jnp.float32),
            pltpu.VMEM((rows, outs) if started else (8, 128), jnp.float32),
            pltpu.SemaphoreType.DMA((count,)),
            pltpu.SemaphoreType.DMA((count,)),
            pltpu.SemaphoreType.DMA,
        ],
        compiler_params=pltpu.CompilerParams(vmem_limit_bytes=60 << 20),
        cost_estimate=pl.CostEstimate(
            flops=2 * rows * outs * sum(widths),
            transcendentals=0,
            bytes_accessed=2 * sum(widths) * (rows + outs) + 8 * rows * outs,
        ),
        name="chunk_matmul",
    )(jnp.stack(blocks).astype(jnp.int32), *pieces, w_down, *old)


def on_device(hidden, out_grad, w_down, proj_in, proj_out, queries, assignment):
    rank = lax.axis_index("tensor")
    core = rank & 1
    z = (rank >> 1) & (ZN - 1)
    xh = rank >> 4
    toward = 1 - 2 * core
    width = out_grad.shape[1]

    def both(own, other):
        return jnp.where(core == 0, jnp.concatenate([own, other], 1), jnp.concatenate([other, own], 1))

    def halve(value, bit, perm):
        half = value.shape[1] // 2
        keep = lax.dynamic_slice_in_dim(value, bit * half, half, 1)
        give = lax.dynamic_slice_in_dim(value, (1 - bit) * half, half, 1)
        return keep + move(give, perm)

    together = lax.optimization_barrier
    pieces = []
    blocks = []

    def keep(column, depth, value):
        pieces.append(value)
        blocks.append(2 * (column * ZN + ((depth + 2 * ZN) & (ZN - 1))))

    def keep_half(column, value, side):
        pieces.append(value)
        blocks.append(2 * (column * ZN + ((z + 4) & (ZN - 1))) + side)

    def flush(total, out_type=jnp.float32):
        total = chunk_matmul(total, pieces, blocks, w_down, out_type)
        pieces.clear()
        blocks.clear()
        return total

    def mine_of(pair):
        return lax.dynamic_slice_in_dim(pair, core * width, width, 1)

    near, far = xh, 1 - xh
    other = move(out_grad, CORE)
    crossed = move(out_grad, ACROSS)
    other, hidden, proj_out = together((other, hidden, proj_out))
    own0 = both(out_grad, other)
    own1 = move(own0, ALONG)
    act_part = mul(hidden, proj_in)
    grad_part = mul(out_grad, proj_out)
    low = jnp.concatenate([act_part, grad_part], 1)
    seq_count = low.shape[0] // LEN
    wide = low.shape[1]
    low = low.reshape(seq_count, LEN, wide)
    low = halve(low, core, CORE)
    low = halve(low, xh, ACROSS)

    far0 = both(crossed, move(crossed, CORE))
    far1 = move(far0, ALONG)
    far0, low = together((far0, low))
    own2 = move(own1, ALONG)
    share = low.shape[1] // ZN
    low = low.reshape(seq_count, ZN, share, wide).transpose(1, 0, 2, 3)
    low = lax.all_to_all(low, "tensor", 0, 0, axis_index_groups=Z_GROUPS, tiled=True)
    low = jnp.sum(low, 0)

    swap1 = move(own1, CORE)
    own1, low = together((own1, low))
    far2 = move(far1, ALONG)
    swapf1 = move(far1, CORE)
    low = jnp.broadcast_to(low[None], (ZN,) + low.shape)
    low = lax.all_to_all(low, "tensor", 0, 0, axis_index_groups=Z_GROUPS, tiled=True)
    low = low.transpose(1, 0, 2, 3).reshape(seq_count, ZN * share, wide)
    half = wide // 2
    seq_grads = jnp.einsum(
        "slk,slm->skm", low[:, :, :half], low[:, :, half:], precision=lax.Precision.HIGHEST
    ).reshape(seq_count, half * half)
    first_seq = lax.axis_index("dp") * seq_count
    mine = lax.dynamic_slice_in_dim(assignment, first_seq, seq_count, 0)
    ids = jnp.arange(DP * EX_DEV, dtype=jnp.int32)
    one_hot = (ids[:, None] == mine[None, :]).astype(jnp.float32)
    sent = jnp.sum(one_hot[:, :, None] * seq_grads[None], 1)
    sent = sent.reshape(DP, EX_DEV, half * half)

    far1, sent = together((far1, sent))
    own3 = move(own2, ALONG)
    swap2 = move(own2, CORE)
    got = lax.all_to_all(sent, "dp", 0, 0, tiled=True)
    keep(near, z, own0)
    keep(far, z, far0)
    keep(near, z - toward, own1)
    keep(near, z + toward, swap1)
    keep(far, z - toward, far1)
    keep(far, z + toward, swapf1)
    total = flush(None)
    got, total = together((got, total))
    far3 = move(far2, ALONG)
    swapf2 = move(far2, CORE)
    example_grads = jnp.sum(got, 0)

    own2, example_grads = together((own2, example_grads))
    own4 = move(mine_of(own3), ALONG)
    swap3 = move(own3, CORE)
    example_grads = example_grads + move(example_grads, ACROSS)
    example_grads = example_grads + move(example_grads, CORE)
    scores = jnp.dot(example_grads, queries.astype(jnp.float32).T, precision=lax.Precision.HIGHEST)

    far2, scores = together((far2, scores))
    far4 = move(mine_of(far3), ALONG)
    swapf3 = move(far3, CORE)
    keep(near, z - 2 * toward, own2)
    keep(near, z + 2 * toward, swap2)
    keep(far, z - 2 * toward, far2)
    keep(far, z + 2 * toward, swapf2)
    keep(near, z - 3 * toward, own3)
    keep(near, z + 3 * toward, swap3)
    total = flush(total)
    far4, own4, total = together((far4, own4, total))
    swap4 = move(own4, CORE)
    swapf4 = move(far4, CORE)
    keep(far, z - 3 * toward, far3)
    keep(far, z + 3 * toward, swapf3)
    keep_half(near, own4, core)
    keep_half(near, swap4, 1 - core)
    keep_half(far, far4, core)
    keep_half(far, swapf4, 1 - core)
    total = flush(total, jnp.bfloat16)
    return (total, scores)


def solution(mesh):
    placed = (
        P("dp", "tensor"),
        P("dp", "tensor"),
        P("tensor", None),
        P(None, "tensor"),
        P(None, "tensor"),
        P("tensor", None),
        P(),
    )
    return jax.shard_map(
        on_device,
        mesh=mesh,
        in_specs=placed,
        out_specs=(P("dp", "tensor"), P("dp", "tensor")),
        check_vma=False,
    )
```
